512 devices in a mesh: rep: 16 (over y_hi, x, core), shard: 32 (over y_lo, z).
Axes of the slice: x: 4, y: 8 (y_hi: 2, y_lo: 4; y = y_hi * 4 + y_lo), z: 8, core: 2. Of those that a mesh axis runs over, the one named last changes fastest.
Arguments:
- grad_blocks: float32 [16, 1664, 2048], P('rep', None, 'shard'), may hold values from -2400 to 2400
- gain_grads: float32 [16, 12800], P('rep', 'shard'), may hold values from -240 to 240
- first_moment: float32 [32, 106896], P('shard'), may hold values from -6 to 6
- second_moment: float32 [32, 106896], P('shard'), may hold values from 0.25 to 4
- master_flat: float32 [32, 106896], P('shard'), may hold values from -6 to 6
- ema_flat: float32 [32, 106896], P('shard'), may hold values from -6 to 6
Outputs:
- new_first: float32 [32, 106896], P('shard')
- new_second: float32 [32, 106896], P('shard')
- new_master: float32 [32, 106896], P('shard')
- new_ema: float32 [32, 106896], P('shard')
- weight_blocks: bfloat16 [2, 1664, 2048], P(None, None, 'shard')
- gains: bfloat16 [12800], replicated
The draws below stay inside these ranges and needn't reach their ends.
All inputs are finite; a program needn't handle non-finite values.
Results may differ from the reference program's by a relative error of at most 0.0004.
Values may be sent and summed in bfloat16 or wider, within the bound.
A program may use at most 64 MiB of HBM per device.

```python
import math
import jax
import jax.numpy as jnp
from jax import lax

D = 2048
STEP = 100
ROWS = 1664
SMALL = 12800
PARAMS = 3420672
REPLICAS = 16
OWNERS = 32
MAIN_DEV = 106496
FLAT_DEV = 106896


def draw_grad_blocks(key, part):
    keys = jax.random.split(key, 3)
    position = jnp.arange(ROWS, dtype=jnp.float32)[:, None] / ROWS
    rising = 3.0 ** position
    row_scale = 10.0 ** jax.random.uniform(keys[0], (ROWS, 1), jnp.float32) * rising
    col_scale = 10.0 ** jax.random.uniform(keys[1], (1, D), jnp.float32)
    noise = jax.random.truncated_normal(keys[2], -4.0, 4.0, (REPLICAS, ROWS, D), jnp.float32)
    amplitude = 2.0
    return amplitude * row_scale[None] * col_scale[None] * noise


def draw_gain_grads(key, part):
    keys = jax.random.split(jax.random.fold_in(key, 7), 2)
    values = 40.0 * jax.random.truncated_normal(keys[1], -6.0, 6.0, (REPLICAS, SMALL), jnp.float32)
    return values


def levels(key, shape, shards, low, high):
    loudness = 1.0
    for axis_at, blocks in shards:
        draws = jax.random.uniform(jax.random.fold_in(jax.random.fold_in(key, 6), axis_at), (blocks,), jnp.float32, low / len(shards), high / len(shards))
        loudness = loudness * jnp.repeat(jnp.exp(draws), shape[axis_at] // blocks).reshape((-1,) + (1,) * (len(shape) - 1 - axis_at))
    return loudness


def normal_values(key, extent, spread, most, cuts=(), held_as=jnp.bfloat16):
    values = spread * jax.random.normal(key, extent, jnp.float32)
    if cuts:
        values = values * levels(key, extent, cuts, -0.22, 0.18)
    return jnp.clip(values, -most, most).astype(held_as)


def setup_inputs(seed: int = 0) -> dict:
    seeds = jax.random.split(jax.random.key(seed), 7)
    grad_blocks = draw_grad_blocks(jax.random.fold_in(seeds[6], 71), 0)
    gain_grads = draw_gain_grads(jax.random.fold_in(seeds[6], 71), 0)
    first_moment = normal_values(seeds[2], (OWNERS, FLAT_DEV), 1.0, 6.0, ((0, 32),), jnp.float32)
    second_moment = jnp.clip(jnp.exp(math.log(4.0) - 2.7725887 * jax.random.uniform(seeds[3], (OWNERS, FLAT_DEV), jnp.float32) ** levels(seeds[3], (OWNERS, FLAT_DEV), ((0, 32),), -0.2, 0.2)), 0.25, 4.0)
    master_flat = normal_values(seeds[4], (OWNERS, FLAT_DEV), 1.0, 6.0, ((0, 32),), jnp.float32)
    ema_flat = normal_values(seeds[5], (OWNERS, FLAT_DEV), 1.0, 6.0, ((0, 32),), jnp.float32)
    return dict(grad_blocks=grad_blocks, gain_grads=gain_grads, first_moment=first_moment, second_moment=second_moment, master_flat=master_flat, ema_flat=ema_flat)


beta_one = 0.9
beta_two = 0.95
adam_eps = 1e-08
learn_rate = 0.02
weight_decay = 0.1
ema_keep = 0.95
clip_eps = 1e-06

def reference(grad_blocks, gain_grads, first_moment, second_moment, master_flat, ema_flat):
    grad_main = lax.optimization_barrier(jnp.sum(grad_blocks, axis=0)) / REPLICAS
    grad_small = lax.optimization_barrier(jnp.sum(gain_grads, axis=0)) / REPLICAS
    owned = jnp.concatenate([grad_main.reshape(OWNERS, MAIN_DEV), grad_small.reshape(OWNERS, SMALL // OWNERS)], axis=1)
    total = jnp.sum(owned * owned)
    rms = jnp.sqrt(total / PARAMS)
    clip = jnp.minimum(1.0, 1.0 / (rms + clip_eps))
    clipped = owned * clip
    new_first = beta_one * first_moment + (1.0 - beta_one) * clipped
    new_second = beta_two * second_moment + (1.0 - beta_two) * clipped * clipped
    update = new_first / (1.0 - beta_one ** STEP) / (jnp.sqrt(new_second / (1.0 - beta_two ** STEP)) + adam_eps)
    column = jnp.arange(FLAT_DEV, dtype=jnp.int32)[None, :]
    decayed = jnp.where(column < MAIN_DEV, weight_decay * master_flat, 0.0)
    new_master = master_flat - learn_rate * (update + decayed)
    new_ema = ema_keep * ema_flat + (1.0 - ema_keep) * new_master
    weights = new_master[:, :MAIN_DEV].reshape(ROWS, D).astype(jnp.bfloat16)
    averaged = new_ema[:, :MAIN_DEV].reshape(ROWS, D).astype(jnp.bfloat16)
    weight_blocks = jnp.stack([weights, averaged], axis=0)
    gains = new_master[:, MAIN_DEV:].reshape(SMALL).astype(jnp.bfloat16)
    return (new_first, new_second, new_master, new_ema, weight_blocks, gains)
```

```python
import jax
import jax.numpy as jnp
from jax import lax
from jax.sharding import PartitionSpec as P

STEP = 100
PARAMS = 3420672


beta_one = 0.9
beta_two = 0.95
adam_eps = 1e-08
learn_rate = 0.02
weight_decay = 0.1
ema_keep = 0.95
clip_eps = 1e-06

LANE = 128


def _pad_to(n):
    return -(-n // LANE) * LANE


def rep_sum(flat, replicas):
    n = flat.shape[0]
    chunk = n // replicas
    width = _pad_to(chunk)
    pieces = jnp.pad(flat.reshape(replicas, chunk), ((0, 0), (0, width - chunk)))
    got = lax.all_to_all(pieces, "rep", split_axis=0, concat_axis=0, tiled=True)
    mine = jnp.sum(got, axis=0)
    every = jnp.broadcast_to(mine[None], (replicas, width))
    full = lax.all_to_all(every, "rep", split_axis=0, concat_axis=0, tiled=True)
    return full[:, :chunk].reshape(n)


def shards(grad_blocks, gain_grads, first_moment, second_moment, master_flat, ema_flat):
    replicas = lax.axis_size("rep")
    owners = lax.axis_size("shard")
    rows, cols = grad_blocks.shape[1], grad_blocks.shape[2]
    small = gain_grads.shape[1]
    main_block = rows * cols
    flat = jnp.concatenate([grad_blocks[0].reshape(main_block), gain_grads[0]])
    summed = rep_sum(flat, replicas)
    matrix_part = summed[:main_block].reshape(rows, cols)
    small_part = summed[main_block:]
    partial_value = jnp.sum(matrix_part * matrix_part) + jnp.sum(small_part * small_part)

    own_rows = rows // owners
    piece = own_rows * cols
    width = _pad_to(piece + 1)
    send = jnp.concatenate(
        [
            matrix_part.reshape(owners, piece),
            jnp.broadcast_to(partial_value, (owners, 1)),
            jnp.zeros((owners, width - piece - 1), jnp.float32),
        ],
        axis=1,
    )
    got = lax.all_to_all(send, "shard", split_axis=0, concat_axis=0, tiled=True)
    total = jnp.sum(got[:, piece]) / (replicas * replicas)
    owned = got[:, :piece].reshape(owners, own_rows, cols).transpose(1, 0, 2)
    main_len = own_rows * owners * cols
    grads = jnp.concatenate([owned.reshape(main_len), small_part]).reshape(1, -1) / replicas
    rms = jnp.sqrt(total / PARAMS)
    clip = jnp.minimum(1.0, 1.0 / (rms + clip_eps))
    clipped = grads * clip
    new_first = beta_one * first_moment + (1.0 - beta_one) * clipped
    new_second = beta_two * second_moment + (1.0 - beta_two) * clipped * clipped
    update = (
        new_first
        / (1.0 - beta_one**STEP)
        / (jnp.sqrt(new_second / (1.0 - beta_two**STEP)) + adam_eps)
    )
    column = jnp.arange(grads.shape[1], dtype=jnp.int32)[None, :]
    decayed = jnp.where(column < main_len, weight_decay * master_flat, 0.0)
    new_master = master_flat - learn_rate * (update + decayed)
    new_ema = ema_keep * ema_flat + (1.0 - ema_keep) * new_master
    weights = new_master[0, :main_len].astype(jnp.bfloat16)
    averaged = new_ema[0, :main_len].astype(jnp.bfloat16)
    stacked = jnp.stack([weights, averaged], axis=0).reshape(2, own_rows, owners, cols)
    back = stacked.transpose(2, 0, 1, 3).reshape(owners, 2 * piece)
    gains_mine = new_master[0, main_len:].astype(jnp.bfloat16)
    width2 = _pad_to(2 * piece + small)
    send2 = jnp.concatenate(
        [
            back,
            jnp.broadcast_to(gains_mine[None], (owners, small)),
            jnp.zeros((owners, width2 - 2 * piece - small), jnp.bfloat16),
        ],
        axis=1,
    )
    got2 = lax.all_to_all(send2, "shard", split_axis=0, concat_axis=0, tiled=True)
    weight_blocks = (
        got2[:, : 2 * piece].reshape(owners, 2, own_rows, cols).transpose(1, 0, 2, 3).reshape(2, rows, cols)
    )
    gains = got2[:, 2 * piece : 2 * piece + small].reshape(owners * small)
    return (new_first, new_second, new_master, new_ema, weight_blocks, gains)


def solution(mesh):
    return jax.shard_map(
        shards,
        mesh=mesh,
        in_specs=(
            P("rep", None, "shard"),
            P("rep", "shard"),
            P("shard", None),
            P("shard", None),
            P("shard", None),
            P("shard", None),
        ),
        out_specs=(
            P("shard", None),
            P("shard", None),
            P("shard", None),
            P("shard", None),
            P(None, None, "shard"),
            P(),
        ),
        check_vma=False,
    )
```

```python
import jax
import jax.numpy as jnp
from jax import lax
from jax.sharding import PartitionSpec as P

STEP = 100
PARAMS = 3420672


beta_one = 0.9
beta_two = 0.95
adam_eps = 1e-08
learn_rate = 0.02
weight_decay = 0.1
ema_keep = 0.95
clip_eps = 1e-06

LANE = 128


def _pad_to(n):
    return -(-n // LANE) * LANE


def shards(grad_blocks, gain_grads, first_moment, second_moment, master_flat, ema_flat):
    replicas = lax.axis_size("rep")
    owners = lax.axis_size("shard")
    me = lax.axis_index("shard")
    rows, cols = grad_blocks.shape[1], grad_blocks.shape[2]
    small = gain_grads.shape[1]
    own_rows = rows // owners
    piece = own_rows * cols
    sub = piece // replicas
    gsub = small // replicas
    block = grad_blocks[0].reshape(owners, replicas, sub).transpose(1, 0, 2).reshape(replicas, owners * sub)
    gains_in = gain_grads[0].reshape(replicas, gsub)
    width = _pad_to(owners * sub + gsub)
    send = jnp.concatenate(
        [block, gains_in, jnp.zeros((replicas, width - owners * sub - gsub), jnp.float32)], axis=1
    )
    got = lax.all_to_all(send, "rep", split_axis=0, concat_axis=0, tiled=True)
    mine = jnp.sum(got, axis=0)
    chunk = mine[: owners * sub].reshape(owners, sub)
    gain_chunk = mine[owners * sub : owners * sub + gsub]
    partial_value = jnp.sum(chunk * chunk) + jnp.sum(gain_chunk * gain_chunk)
    width2 = _pad_to(sub + gsub + 1)
    rowdata = jnp.concatenate(
        [
            chunk,
            jnp.broadcast_to(gain_chunk[None], (owners, gsub)),
            jnp.broadcast_to(partial_value, (owners, 1)),
            jnp.zeros((owners, width2 - sub - gsub - 1), jnp.float32),
        ],
        axis=1,
    )
    send2 = jnp.broadcast_to(rowdata[None], (replicas, owners, width2)).reshape(replicas * owners, width2)
    got2 = lax.all_to_all(send2, ("rep", "shard"), split_axis=0, concat_axis=0, tiled=True)
    got2 = got2.reshape(replicas, owners, width2)
    total = jnp.sum(got2[:, :, sub + gsub]) / (replicas * replicas)
    owned = (
        got2[:, :, :sub].transpose(1, 0, 2).reshape(owners, own_rows, cols).transpose(1, 0, 2)
    )
    small_part = lax.dynamic_index_in_dim(got2[:, :, sub : sub + gsub], me, axis=1, keepdims=False)
    small_part = small_part.reshape(small)
    main_len = own_rows * owners * cols
    grads = jnp.concatenate([owned.reshape(main_len), small_part]).reshape(1, -1) / replicas
    rms = jnp.sqrt(total / PARAMS)
    clip = jnp.minimum(1.0, 1.0 / (rms + clip_eps))
    clipped = grads * clip
    new_first = beta_one * first_moment + (1.0 - beta_one) * clipped
    new_second = beta_two * second_moment + (1.0 - beta_two) * clipped * clipped
    update = (
        new_first
        / (1.0 - beta_one**STEP)
        / (jnp.sqrt(new_second / (1.0 - beta_two**STEP)) + adam_eps)
    )
    column = jnp.arange(grads.shape[1], dtype=jnp.int32)[None, :]
    decayed = jnp.where(column < main_len, weight_decay * master_flat, 0.0)
    new_master = master_flat - learn_rate * (update + decayed)
    new_ema = ema_keep * ema_flat + (1.0 - ema_keep) * new_master
    weights = new_master[0, :main_len].astype(jnp.bfloat16)
    averaged = new_ema[0, :main_len].astype(jnp.bfloat16)
    stacked = jnp.stack([weights, averaged], axis=0).reshape(2, own_rows, owners, cols)
    back = stacked.transpose(2, 0, 1, 3).reshape(owners, 2 * piece)
    gains_mine = new_master[0, main_len:].astype(jnp.bfloat16)
    width2 = _pad_to(2 * piece + small)
    send2 = jnp.concatenate(
        [
            back,
            jnp.broadcast_to(gains_mine[None], (owners, small)),
            jnp.zeros((owners, width2 - 2 * piece - small), jnp.bfloat16),
        ],
        axis=1,
    )
    got2 = lax.all_to_all(send2, "shard", split_axis=0, concat_axis=0, tiled=True)
    weight_blocks = (
        got2[:, : 2 * piece].reshape(owners, 2, own_rows, cols).transpose(1, 0, 2, 3).reshape(2, rows, cols)
    )
    gains = got2[:, 2 * piece : 2 * piece + small].reshape(owners * small)
    return (new_first, new_second, new_master, new_ema, weight_blocks, gains)


def solution(mesh):
    return jax.shard_map(
        shards,
        mesh=mesh,
        in_specs=(
            P("rep", None, "shard"),
            P("rep", "shard"),
            P("shard", None),
            P("shard", None),
            P("shard", None),
            P("shard", None),
        ),
        out_specs=(
            P("shard", None),
            P("shard", None),
            P("shard", None),
            P("shard", None),
            P(None, None, "shard"),
            P(),
        ),
        check_vma=False,
    )
```

```python
import jax
import jax.numpy as jnp
from jax import lax
import functools

from jax.experimental import pallas as pl
from jax.experimental.pallas import tpu as pltpu
from jax.sharding import PartitionSpec as P

STEP = 100
PARAMS = 3420672


beta_one = 0.9
beta_two = 0.95
adam_eps = 1e-08
learn_rate = 0.02
weight_decay = 0.1
ema_keep = 0.95
clip_eps = 1e-06

LANE = 128
TILE = {jnp.dtype(jnp.float32): 8 * LANE, jnp.dtype(jnp.bfloat16): 16 * LANE}


def _pad_to(n, dtype=jnp.float32):
    unit = TILE[jnp.dtype(dtype)]
    return -(-n // unit) * unit


MESH = pl.DeviceIdType.MESH


def _a2a_kernel(axis, other_axis, n, x_ref, y_ref, send_sem, recv_sem, local_sem):
    me = lax.axis_index(axis)
    other = lax.axis_index(other_axis)

    def dev(j):
        return (other, j) if axis == "shard" else (j, other)

    barrier = pltpu.get_barrier_semaphore()
    for k in range(1, n):
        pl.semaphore_signal(barrier, inc=1, device_id=dev(lax.rem(me + k, n)), device_id_type=MESH)
    pl.semaphore_wait(barrier, n - 1)
    local = pltpu.make_async_copy(x_ref.at[me], y_ref.at[me], local_sem)
    local.start()
    for k in range(1, n):
        j = lax.rem(me + k, n)
        pltpu.make_async_remote_copy(
            src_ref=x_ref.at[j],
            dst_ref=y_ref.at[me],
            send_sem=send_sem.at[k],
            recv_sem=recv_sem.at[k],
            device_id=dev(j),
            device_id_type=MESH,
        ).start()
    local.wait()
    for k in range(1, n):
        j = lax.rem(me + k, n)
        src = lax.rem(me + n - k, n)
        pltpu.make_async_remote_copy(
            src_ref=x_ref.at[j],
            dst_ref=y_ref.at[src],
            send_sem=send_sem.at[k],
            recv_sem=recv_sem.at[k],
            device_id=dev(j),
            device_id_type=MESH,
        ).wait_send()
        pltpu.make_async_remote_copy(
            src_ref=x_ref.at[j],
            dst_ref=y_ref.at[src],
            send_sem=send_sem.at[k],
            recv_sem=recv_sem.at[k],
            device_id=dev(j),
            device_id_type=MESH,
        ).wait_recv()


def all_to_all(x, axis, other_axis, n, collective_id):
    return pl.pallas_call(
        functools.partial(_a2a_kernel, axis, other_axis, n),
        out_shape=jax.ShapeDtypeStruct(x.shape, x.dtype),
        in_specs=[pl.BlockSpec(memory_space=pl.ANY)],
        out_specs=pl.BlockSpec(memory_space=pl.ANY),
        scratch_shapes=[
            pltpu.SemaphoreType.DMA((n,)),
            pltpu.SemaphoreType.DMA((n,)),
            pltpu.SemaphoreType.DMA,
        ],
        compiler_params=pltpu.CompilerParams(collective_id=collective_id, has_side_effects=True),
    )(x)


def exchange(pieces, axis, collective_id):
    other = "rep" if axis == "shard" else "shard"
    n, width = pieces.shape
    got = all_to_all(pieces.reshape(n, width // LANE, LANE), axis, other, n, collective_id)
    return got.reshape(n, width)


def rep_sum(flat, replicas):
    n = flat.shape[0]
    chunk = n // replicas
    width = _pad_to(chunk)
    pieces = jnp.pad(flat.reshape(replicas, chunk), ((0, 0), (0, width - chunk)))
    got = exchange(pieces, "rep", 0)
    mine = jnp.sum(got, axis=0)
    every = jnp.broadcast_to(mine[None], (replicas, width))
    full = exchange(every, "rep", 1)
    return full[:, :chunk].reshape(n)


def shards(grad_blocks, gain_grads, first_moment, second_moment, master_flat, ema_flat):
    replicas = lax.axis_size("rep")
    owners = lax.axis_size("shard")
    rows, cols = grad_blocks.shape[1], grad_blocks.shape[2]
    small = gain_grads.shape[1]
    main_block = rows * cols
    flat = jnp.concatenate([grad_blocks[0].reshape(main_block), gain_grads[0]])
    summed = rep_sum(flat, replicas)
    matrix_part = summed[:main_block].reshape(rows, cols)
    small_part = summed[main_block:]
    partial_value = jnp.sum(matrix_part * matrix_part) + jnp.sum(small_part * small_part)

    own_rows = rows // owners
    piece = own_rows * cols
    width = _pad_to(piece + 1)
    send = jnp.concatenate(
        [
            matrix_part.reshape(owners, piece),
            jnp.broadcast_to(partial_value, (owners, 1)),
            jnp.zeros((owners, width - piece - 1), jnp.float32),
        ],
        axis=1,
    )
    got = exchange(send, "shard", 2)
    total = jnp.sum(got[:, piece]) / (replicas * replicas)
    owned = got[:, :piece].reshape(owners, own_rows, cols).transpose(1, 0, 2)
    main_len = own_rows * owners * cols
    grads = jnp.concatenate([owned.reshape(main_len), small_part]).reshape(1, -1) / replicas
    rms = jnp.sqrt(total / PARAMS)
    clip = jnp.minimum(1.0, 1.0 / (rms + clip_eps))
    clipped = grads * clip
    new_first = beta_one * first_moment + (1.0 - beta_one) * clipped
    new_second = beta_two * second_moment + (1.0 - beta_two) * clipped * clipped
    update = (
        new_first
        / (1.0 - beta_one**STEP)
        / (jnp.sqrt(new_second / (1.0 - beta_two**STEP)) + adam_eps)
    )
    column = jnp.arange(grads.shape[1], dtype=jnp.int32)[None, :]
    decayed = jnp.where(column < main_len, weight_decay * master_flat, 0.0)
    new_master = master_flat - learn_rate * (update + decayed)
    new_ema = ema_keep * ema_flat + (1.0 - ema_keep) * new_master
    weights = new_master[0, :main_len].astype(jnp.bfloat16)
    averaged = new_ema[0, :main_len].astype(jnp.bfloat16)
    stacked = jnp.stack([weights, averaged], axis=0).reshape(2, own_rows, owners, cols)
    back = stacked.transpose(2, 0, 1, 3).reshape(owners, 2 * piece)
    gains_mine = new_master[0, main_len:].astype(jnp.bfloat16)
    width2 = _pad_to(2 * piece + small, jnp.bfloat16)
    send2 = jnp.concatenate(
        [
            back,
            jnp.broadcast_to(gains_mine[None], (owners, small)),
            jnp.zeros((owners, width2 - 2 * piece - small), jnp.bfloat16),
        ],
        axis=1,
    )
    got2 = exchange(send2, "shard", 3)
    weight_blocks = (
        got2[:, : 2 * piece].reshape(owners, 2, own_rows, cols).transpose(1, 0, 2, 3).reshape(2, rows, cols)
    )
    gains = got2[:, 2 * piece : 2 * piece + small].reshape(owners * small)
    return (new_first, new_second, new_master, new_ema, weight_blocks, gains)


def solution(mesh):
    return jax.shard_map(
        shards,
        mesh=mesh,
        in_specs=(
            P("rep", None, "shard"),
            P("rep", "shard"),
            P("shard", None),
            P("shard", None),
            P("shard", None),
            P("shard", None),
        ),
        out_specs=(
            P("shard", None),
            P("shard", None),
            P("shard", None),
            P("shard", None),
            P(None, None, "shard"),
            P(),
        ),
        check_vma=False,
    )
```

```python
import jax
import jax.numpy as jnp
from jax import lax
import functools

from jax.experimental import pallas as pl
from jax.experimental.pallas import tpu as pltpu
from jax.sharding import PartitionSpec as P

STEP = 100
PARAMS = 3420672


beta_one = 0.9
beta_two = 0.95
adam_eps = 1e-08
learn_rate = 0.02
weight_decay = 0.1
ema_keep = 0.95
clip_eps = 1e-06

LANE = 128
TILE = {jnp.dtype(jnp.float32): 8 * LANE, jnp.dtype(jnp.bfloat16): 16 * LANE}


def _pad_to(n, dtype=jnp.float32):
    unit = TILE[jnp.dtype(dtype)]
    return -(-n // unit) * unit


MESH = pl.DeviceIdType.MESH


def _a2a_kernel(axis, other_axis, stride, n, x_ref, y_ref, send_sem, recv_sem, local_sem):
    me = lax.axis_index(axis)
    other = lax.axis_index(other_axis)
    pos = lax.rem(lax.div(me, stride), n)
    base = me - pos * stride

    def dev(j):
        index = base + j * stride
        return (other, index) if axis == "shard" else (index, other)

    barrier = pltpu.get_barrier_semaphore()
    for k in range(1, n):
        pl.semaphore_signal(barrier, inc=1, device_id=dev(lax.rem(pos + k, n)), device_id_type=MESH)
    pl.semaphore_wait(barrier, n - 1)
    local = pltpu.make_async_copy(x_ref.at[pos], y_ref.at[pos], local_sem)
    local.start()
    for k in range(1, n):
        j = lax.rem(pos + k, n)
        pltpu.make_async_remote_copy(
            src_ref=x_ref.at[j],
            dst_ref=y_ref.at[pos],
            send_sem=send_sem.at[k],
            recv_sem=recv_sem.at[k],
            device_id=dev(j),
            device_id_type=MESH,
        ).start()
    local.wait()
    for k in range(1, n):
        j = lax.rem(pos + k, n)
        src = lax.rem(pos + n - k, n)
        copy = pltpu.make_async_remote_copy(
            src_ref=x_ref.at[j],
            dst_ref=y_ref.at[src],
            send_sem=send_sem.at[k],
            recv_sem=recv_sem.at[k],
            device_id=dev(j),
            device_id_type=MESH,
        )
        copy.wait_send()
        copy.wait_recv()


def all_to_all(x, axis, other_axis, stride, collective_id):
    n = x.shape[0]
    return pl.pallas_call(
        functools.partial(_a2a_kernel, axis, other_axis, stride, n),
        out_shape=jax.ShapeDtypeStruct(x.shape, x.dtype),
        in_specs=[pl.BlockSpec(memory_space=pl.ANY)],
        out_specs=pl.BlockSpec(memory_space=pl.ANY),
        scratch_shapes=[
            pltpu.SemaphoreType.DMA((n,)),
            pltpu.SemaphoreType.DMA((n,)),
            pltpu.SemaphoreType.DMA,
        ],
        compiler_params=pltpu.CompilerParams(collective_id=collective_id, has_side_effects=True),
    )(x)


def exchange(pieces, axis, collective_id, stride=1):
    other = "rep" if axis == "shard" else "shard"
    n, width = pieces.shape
    got = all_to_all(pieces.reshape(n, width // LANE, LANE), axis, other, stride, collective_id)
    return got.reshape(n, width)


def rep_sum(flat, replicas):
    cores = 2
    chips = replicas // cores
    n = flat.shape[0]
    quarter = -(-n // replicas)
    width = _pad_to(quarter)
    padded = jnp.pad(flat, (0, width * replicas - n)).reshape(cores, chips * width)
    half = jnp.sum(exchange(padded, "rep", 0, 1), axis=0)
    mine = jnp.sum(exchange(half.reshape(chips, width), "rep", 1, cores), axis=0)
    every = exchange(jnp.broadcast_to(mine[None], (chips, width)), "rep", 4, cores)
    whole = exchange(jnp.broadcast_to(every.reshape(1, chips * width), (cores, chips * width)), "rep", 5, 1)
    return whole.reshape(cores * chips * width)[:n]


def shards(grad_blocks, gain_grads, first_moment, second_moment, master_flat, ema_flat):
    replicas = lax.axis_size("rep")
    owners = lax.axis_size("shard")
    rows, cols = grad_blocks.shape[1], grad_blocks.shape[2]
    small = gain_grads.shape[1]
    main_block = rows * cols
    flat = jnp.concatenate([grad_blocks[0].reshape(main_block), gain_grads[0]])
    summed = rep_sum(flat, replicas)
    matrix_part = summed[:main_block].reshape(rows, cols)
    small_part = summed[main_block:]
    partial_value = jnp.sum(matrix_part * matrix_part) + jnp.sum(small_part * small_part)

    own_rows = rows // owners
    piece = own_rows * cols
    width = _pad_to(piece + 1)
    send = jnp.concatenate(
        [
            matrix_part.reshape(owners, piece),
            jnp.broadcast_to(partial_value, (owners, 1)),
            jnp.zeros((owners, width - piece - 1), jnp.float32),
        ],
        axis=1,
    )
    got = exchange(send, "shard", 2)
    total = jnp.sum(got[:, piece]) / (replicas * replicas)
    owned = got[:, :piece].reshape(owners, own_rows, cols).transpose(1, 0, 2)
    main_len = own_rows * owners * cols
    grads = jnp.concatenate([owned.reshape(main_len), small_part]).reshape(1, -1) / replicas
    rms = jnp.sqrt(total / PARAMS)
    clip = jnp.minimum(1.0, 1.0 / (rms + clip_eps))
    clipped = grads * clip
    new_first = beta_one * first_moment + (1.0 - beta_one) * clipped
    new_second = beta_two * second_moment + (1.0 - beta_two) * clipped * clipped
    update = (
        new_first
        / (1.0 - beta_one**STEP)
        / (jnp.sqrt(new_second / (1.0 - beta_two**STEP)) + adam_eps)
    )
    column = jnp.arange(grads.shape[1], dtype=jnp.int32)[None, :]
    decayed = jnp.where(column < main_len, weight_decay * master_flat, 0.0)
    new_master = master_flat - learn_rate * (update + decayed)
    new_ema = ema_keep * ema_flat + (1.0 - ema_keep) * new_master
    weights = new_master[0, :main_len].astype(jnp.bfloat16)
    averaged = new_ema[0, :main_len].astype(jnp.bfloat16)
    stacked = jnp.stack([weights, averaged], axis=0).reshape(2, own_rows, owners, cols)
    back = stacked.transpose(2, 0, 1, 3).reshape(owners, 2 * piece)
    gains_mine = new_master[0, main_len:].astype(jnp.bfloat16)
    width2 = _pad_to(2 * piece + small, jnp.bfloat16)
    send2 = jnp.concatenate(
        [
            back,
            jnp.broadcast_to(gains_mine[None], (owners, small)),
            jnp.zeros((owners, width2 - 2 * piece - small), jnp.bfloat16),
        ],
        axis=1,
    )
    got2 = exchange(send2, "shard", 3)
    weight_blocks = (
        got2[:, : 2 * piece].reshape(owners, 2, own_rows, cols).transpose(1, 0, 2, 3).reshape(2, rows, cols)
    )
    gains = got2[:, 2 * piece : 2 * piece + small].reshape(owners * small)
    return (new_first, new_second, new_master, new_ema, weight_blocks, gains)


def solution(mesh):
    return jax.shard_map(
        shards,
        mesh=mesh,
        in_specs=(
            P("rep", None, "shard"),
            P("rep", "shard"),
            P("shard", None),
            P("shard", None),
            P("shard", None),
            P("shard", None),
        ),
        out_specs=(
            P("shard", None),
            P("shard", None),
            P("shard", None),
            P("shard", None),
            P(None, None, "shard"),
            P(),
        ),
        check_vma=False,
    )
```

```python
import jax
import jax.numpy as jnp
from jax import lax
from jax.sharding import PartitionSpec as P

STEP = 100
PARAMS = 3420672


beta_one = 0.9
beta_two = 0.95
adam_eps = 1e-08
learn_rate = 0.02
weight_decay = 0.1
ema_keep = 0.95
clip_eps = 1e-06

LANE = 128


def _pad_to(n):
    return -(-n // LANE) * LANE


def shards(grad_blocks, gain_grads, first_moment, second_moment, master_flat, ema_flat):
    replicas = lax.axis_size("rep")
    owners = lax.axis_size("shard")
    me = lax.axis_index("shard")
    rows, cols = grad_blocks.shape[1], grad_blocks.shape[2]
    small = gain_grads.shape[1]
    own_rows = rows // owners
    piece = own_rows * cols
    sub = piece // replicas
    gsub = small // replicas
    block = grad_blocks[0].reshape(owners, replicas, sub).transpose(1, 0, 2).reshape(replicas, owners * sub)
    gains_in = gain_grads[0].reshape(replicas, gsub)
    width = _pad_to(owners * sub + gsub)
    send = jnp.pad(jnp.concatenate([block, gains_in], axis=1), ((0, 0), (0, width - owners * sub - gsub)))
    got = lax.all_to_all(send, "rep", split_axis=0, concat_axis=0, tiled=True)
    mine = jnp.sum(got, axis=0)
    chunk = mine[: owners * sub].reshape(owners, sub)
    gain_chunk = mine[owners * sub : owners * sub + gsub]
    partial_value = jnp.sum(chunk * chunk) + jnp.sum(gain_chunk * gain_chunk)
    width2 = _pad_to(sub + gsub + 1)
    rowdata = jnp.pad(
        jnp.concatenate(
            [
                chunk,
                jnp.broadcast_to(gain_chunk[None], (owners, gsub)),
                jnp.broadcast_to(partial_value, (owners, 1)),
            ],
            axis=1,
        ),
        ((0, 0), (0, width2 - sub - gsub - 1)),
    )
    send2 = jnp.broadcast_to(rowdata[None], (replicas, owners, width2)).reshape(replicas * owners, width2)
    got2 = lax.all_to_all(send2, ("rep", "shard"), split_axis=0, concat_axis=0, tiled=True)
    got2 = got2.reshape(replicas, owners, width2)
    total = jnp.sum(got2[:, :, sub + gsub]) / (replicas * replicas)
    owned = (
        got2[:, :, :sub].transpose(1, 0, 2).reshape(owners, own_rows, cols).transpose(1, 0, 2)
    )
    small_part = lax.dynamic_index_in_dim(got2[:, :, sub : sub + gsub], me, axis=1, keepdims=False)
    small_part = small_part.reshape(small)
    main_len = own_rows * owners * cols
    grads = jnp.concatenate([owned.reshape(main_len), small_part]).reshape(1, -1)
    rms = jnp.sqrt(total / PARAMS)
    clip = jnp.minimum(1.0, 1.0 / (rms + clip_eps))
    clipped = grads * (clip / replicas)
    new_first = beta_one * first_moment + (1.0 - beta_one) * clipped
    new_second = beta_two * second_moment + (1.0 - beta_two) * clipped * clipped
    update = (
        new_first
        / (1.0 - beta_one**STEP)
        / (jnp.sqrt(new_second / (1.0 - beta_two**STEP)) + adam_eps)
    )
    column = jnp.arange(grads.shape[1], dtype=jnp.int32)[None, :]
    decayed = jnp.where(column < main_len, weight_decay * master_flat, 0.0)
    new_master = master_flat - learn_rate * (update + decayed)
    new_ema = ema_keep * ema_flat + (1.0 - ema_keep) * new_master
    weights = new_master[0, :main_len].astype(jnp.bfloat16)
    averaged = new_ema[0, :main_len].astype(jnp.bfloat16)
    stacked = jnp.stack([weights, averaged], axis=0).reshape(2, own_rows, owners, cols)
    back = stacked.transpose(2, 0, 1, 3).reshape(owners, 2 * piece)
    gains_mine = new_master[0, main_len:].astype(jnp.bfloat16)
    width2 = _pad_to(2 * piece + small)
    send2 = jnp.pad(
        jnp.concatenate([back, jnp.broadcast_to(gains_mine[None], (owners, small))], axis=1),
        ((0, 0), (0, width2 - 2 * piece - small)),
    )
    got2 = lax.all_to_all(send2, "shard", split_axis=0, concat_axis=0, tiled=True)
    weight_blocks = (
        got2[:, : 2 * piece].reshape(owners, 2, own_rows, cols).transpose(1, 0, 2, 3).reshape(2, rows, cols)
    )
    gains = got2[:, 2 * piece : 2 * piece + small].reshape(owners * small)
    return (new_first, new_second, new_master, new_ema, weight_blocks, gains)


def solution(mesh):
    return jax.shard_map(
        shards,
        mesh=mesh,
        in_specs=(
            P("rep", None, "shard"),
            P("rep", "shard"),
            P("shard", None),
            P("shard", None),
            P("shard", None),
            P("shard", None),
        ),
        out_specs=(
            P("shard", None),
            P("shard", None),
            P("shard", None),
            P("shard", None),
            P(None, None, "shard"),
            P(),
        ),
        check_vma=False,
    )
```

```python
import jax
import jax.numpy as jnp
from jax import lax
import functools

from jax.experimental import pallas as pl
from jax.experimental.pallas import tpu as pltpu
from jax.sharding import PartitionSpec as P

MESH = pl.DeviceIdType.MESH

STEP = 100
PARAMS = 3420672


beta_one = 0.9
beta_two = 0.95
adam_eps = 1e-08
learn_rate = 0.02
weight_decay = 0.1
ema_keep = 0.95
clip_eps = 1e-06

LANE = 128


def _pad_to(n):
    return -(-n // LANE) * LANE


def _rs_kernel(n, main_rows, tail, x_ref, o_ref, p_ref, recv, send_sem, recv_sem, local_sem):
    me = lax.axis_index("rep")
    shard = lax.axis_index("shard")
    barrier = pltpu.get_barrier_semaphore()
    for k in range(1, n):
        pl.semaphore_signal(barrier, inc=1, device_id=(lax.rem(me + k, n), shard), device_id_type=MESH)
    pl.semaphore_wait(barrier, n - 1)
    local = pltpu.make_async_copy(x_ref.at[me], recv.at[me], local_sem)
    local.start()

    def copy(k, j, src):
        return pltpu.make_async_remote_copy(
            src_ref=x_ref.at[j],
            dst_ref=recv.at[src],
            send_sem=send_sem.at[k],
            recv_sem=recv_sem.at[k],
            device_id=(j, shard),
            device_id_type=MESH,
        )

    for k in range(1, n):
        copy(k, lax.rem(me + k, n), me).start()
    local.wait()
    for k in range(1, n):
        c = copy(k, lax.rem(me + k, n), lax.rem(me + n - k, n))
        c.wait_send()
        c.wait_recv()
    total = recv[0]
    for k in range(1, n):
        total = total + recv[k]
    o_ref[...] = total
    row = lax.broadcasted_iota(jnp.int32, total.shape, 0)
    lane = lax.broadcasted_iota(jnp.int32, total.shape, 1)
    keep = (row < main_rows) | ((row == main_rows) & (lane < tail))
    squares = jnp.where(keep, total * total, 0.0)
    p_ref[...] = jnp.broadcast_to(jnp.sum(squares), p_ref.shape)


def reduce_scatter(x, used, collective_id):
    n, rows, lanes = x.shape
    return pl.pallas_call(
        functools.partial(_rs_kernel, n, used // lanes, used % lanes),
        out_shape=(
            jax.ShapeDtypeStruct((rows, lanes), x.dtype),
            jax.ShapeDtypeStruct((8, lanes), x.dtype),
        ),
        in_specs=[pl.BlockSpec(memory_space=pl.ANY)],
        out_specs=(pl.BlockSpec(memory_space=pltpu.VMEM), pl.BlockSpec(memory_space=pltpu.VMEM)),
        scratch_shapes=[
            pltpu.VMEM((n, rows, lanes), x.dtype),
            pltpu.SemaphoreType.DMA((n,)),
            pltpu.SemaphoreType.DMA((n,)),
            pltpu.SemaphoreType.DMA,
        ],
        compiler_params=pltpu.CompilerParams(collective_id=collective_id, has_side_effects=True),
    )(x)


def shards(grad_blocks, gain_grads, first_moment, second_moment, master_flat, ema_flat):
    replicas = lax.axis_size("rep")
    owners = lax.axis_size("shard")
    me = lax.axis_index("shard")
    rows, cols = grad_blocks.shape[1], grad_blocks.shape[2]
    small = gain_grads.shape[1]
    own_rows = rows // owners
    piece = own_rows * cols
    sub = piece // replicas
    gsub = small // replicas
    block = grad_blocks[0].reshape(owners, replicas, sub).transpose(1, 0, 2).reshape(replicas, owners * sub)
    gains_in = gain_grads[0].reshape(replicas, gsub)
    width = -(-(owners * sub + gsub) // (8 * LANE)) * 8 * LANE
    send = jnp.pad(jnp.concatenate([block, gains_in], axis=1), ((0, 0), (0, width - owners * sub - gsub)))
    mine, partial = reduce_scatter(send.reshape(replicas, width // LANE, LANE), owners * sub + gsub, 0)
    mine = mine.reshape(width)
    chunk = mine[: owners * sub].reshape(owners, sub)
    gain_chunk = mine[owners * sub : owners * sub + gsub]
    partial_value = partial[0, 0]
    width2 = _pad_to(sub + gsub + 1)
    rowdata = jnp.pad(
        jnp.concatenate(
            [
                chunk,
                jnp.broadcast_to(gain_chunk[None], (owners, gsub)),
                jnp.broadcast_to(partial_value, (owners, 1)),
            ],
            axis=1,
        ),
        ((0, 0), (0, width2 - sub - gsub - 1)),
    )
    send2 = jnp.broadcast_to(rowdata[None], (replicas, owners, width2)).reshape(replicas * owners, width2)
    got2 = lax.all_to_all(send2, ("rep", "shard"), split_axis=0, concat_axis=0, tiled=True)
    got2 = got2.reshape(replicas, owners, width2)
    total = jnp.sum(got2[:, :, sub + gsub]) / (replicas * replicas)
    owned = (
        got2[:, :, :sub].transpose(1, 0, 2).reshape(owners, own_rows, cols).transpose(1, 0, 2)
    )
    small_part = lax.dynamic_index_in_dim(got2[:, :, sub : sub + gsub], me, axis=1, keepdims=False)
    small_part = small_part.reshape(small)
    main_len = own_rows * owners * cols
    grads = jnp.concatenate([owned.reshape(main_len), small_part]).reshape(1, -1)
    rms = jnp.sqrt(total / PARAMS)
    clip = jnp.minimum(1.0, 1.0 / (rms + clip_eps))
    clipped = grads * (clip / replicas)
    new_first = beta_one * first_moment + (1.0 - beta_one) * clipped
    new_second = beta_two * second_moment + (1.0 - beta_two) * clipped * clipped
    update = (
        new_first
        / (1.0 - beta_one**STEP)
        / (jnp.sqrt(new_second / (1.0 - beta_two**STEP)) + adam_eps)
    )
    column = jnp.arange(grads.shape[1], dtype=jnp.int32)[None, :]
    decayed = jnp.where(column < main_len, weight_decay * master_flat, 0.0)
    new_master = master_flat - learn_rate * (update + decayed)
    new_ema = ema_keep * ema_flat + (1.0 - ema_keep) * new_master
    weights = new_master[0, :main_len].astype(jnp.bfloat16)
    averaged = new_ema[0, :main_len].astype(jnp.bfloat16)
    stacked = jnp.stack([weights, averaged], axis=0).reshape(2, own_rows, owners, cols)
    back = stacked.transpose(2, 0, 1, 3).reshape(owners, 2 * piece)
    gains_mine = new_master[0, main_len:].astype(jnp.bfloat16)
    width2 = _pad_to(2 * piece + small)
    send2 = jnp.pad(
        jnp.concatenate([back, jnp.broadcast_to(gains_mine[None], (owners, small))], axis=1),
        ((0, 0), (0, width2 - 2 * piece - small)),
    )
    got2 = lax.all_to_all(send2, "shard", split_axis=0, concat_axis=0, tiled=True)
    weight_blocks = (
        got2[:, : 2 * piece].reshape(owners, 2, own_rows, cols).transpose(1, 0, 2, 3).reshape(2, rows, cols)
    )
    gains = got2[:, 2 * piece : 2 * piece + small].reshape(owners * small)
    return (new_first, new_second, new_master, new_ema, weight_blocks, gains)


def solution(mesh):
    return jax.shard_map(
        shards,
        mesh=mesh,
        in_specs=(
            P("rep", None, "shard"),
            P("rep", "shard"),
            P("shard", None),
            P("shard", None),
            P("shard", None),
            P("shard", None),
        ),
        out_specs=(
            P("shard", None),
            P("shard", None),
            P("shard", None),
            P("shard", None),
            P(None, None, "shard"),
            P(),
        ),
        check_vma=False,
    )
```

```python
import jax
import jax.numpy as jnp
from jax import lax
import functools

from jax.experimental import pallas as pl
from jax.experimental.pallas import tpu as pltpu
from jax.sharding import PartitionSpec as P

MESH = pl.DeviceIdType.MESH

STEP = 100
PARAMS = 3420672


beta_one = 0.9
beta_two = 0.95
adam_eps = 1e-08
learn_rate = 0.02
weight_decay = 0.1
ema_keep = 0.95
clip_eps = 1e-06

LANE = 128


def _pad_to(n):
    return -(-n // LANE) * LANE


def _rs_kernel(n, main, share, x_ref, o_ref, p_ref, recv, send_sem, recv_sem, local_sem):
    me = lax.axis_index("rep")
    shard = lax.axis_index("shard")
    barrier = pltpu.get_barrier_semaphore()
    for k in range(1, n):
        pl.semaphore_signal(barrier, inc=1, device_id=(lax.rem(me + k, n), shard), device_id_type=MESH)
    pl.semaphore_wait(barrier, n - 1)
    local = pltpu.make_async_copy(x_ref.at[me], recv.at[me], local_sem)
    local.start()

    def copy(k, j, src):
        return pltpu.make_async_remote_copy(
            src_ref=x_ref.at[j],
            dst_ref=recv.at[src],
            send_sem=send_sem.at[k],
            recv_sem=recv_sem.at[k],
            device_id=(j, shard),
            device_id_type=MESH,
        )

    for k in range(1, n):
        copy(k, lax.rem(me + k, n), me).start()
    local.wait()
    for k in range(1, n):
        c = copy(k, lax.rem(me + k, n), lax.rem(me + n - k, n))
        c.wait_send()
        c.wait_recv()
    total = recv[0]
    for k in range(1, n):
        total = total + recv[k]
    o_ref[...] = total
    flat = (
        lax.broadcasted_iota(jnp.int32, total.shape, 0) * total.shape[1]
        + lax.broadcasted_iota(jnp.int32, total.shape, 1)
    )
    start = main + me * share
    keep = (flat < main) | ((flat >= start) & (flat < start + share))
    squares = jnp.where(keep, total * total, 0.0)
    p_ref[...] = jnp.broadcast_to(jnp.sum(squares), p_ref.shape)


def reduce_scatter(x, main, share, collective_id):
    n, rows, lanes = x.shape
    return pl.pallas_call(
        functools.partial(_rs_kernel, n, main, share),
        out_shape=(
            jax.ShapeDtypeStruct((rows, lanes), x.dtype),
            jax.ShapeDtypeStruct((8, lanes), x.dtype),
        ),
        in_specs=[pl.BlockSpec(memory_space=pl.ANY)],
        out_specs=(pl.BlockSpec(memory_space=pltpu.VMEM), pl.BlockSpec(memory_space=pltpu.VMEM)),
        scratch_shapes=[
            pltpu.VMEM((n, rows, lanes), x.dtype),
            pltpu.SemaphoreType.DMA((n,)),
            pltpu.SemaphoreType.DMA((n,)),
            pltpu.SemaphoreType.DMA,
        ],
        compiler_params=pltpu.CompilerParams(collective_id=collective_id, has_side_effects=True),
    )(x)


def shards(grad_blocks, gain_grads, first_moment, second_moment, master_flat, ema_flat):
    replicas = lax.axis_size("rep")
    owners = lax.axis_size("shard")
    me = lax.axis_index("shard")
    rows, cols = grad_blocks.shape[1], grad_blocks.shape[2]
    small = gain_grads.shape[1]
    own_rows = rows // owners
    piece = own_rows * cols
    sub = piece // replicas
    gsub = small // replicas
    block = grad_blocks[0].reshape(owners, replicas, sub).transpose(1, 0, 2).reshape(replicas, owners * sub)
    gains_in = jnp.broadcast_to(gain_grads, (replicas, small))
    width = -(-(owners * sub + small) // (8 * LANE)) * 8 * LANE
    send = jnp.pad(jnp.concatenate([block, gains_in], axis=1), ((0, 0), (0, width - owners * sub - small)))
    mine, partial = reduce_scatter(send.reshape(replicas, width // LANE, LANE), owners * sub, gsub, 0)
    mine = mine.reshape(width)
    chunk = mine[: owners * sub].reshape(owners, sub)
    small_part = mine[owners * sub : owners * sub + small]
    partial_value = partial[0, 0]
    width2 = _pad_to(sub + 1)
    rowdata = jnp.pad(
        jnp.concatenate([chunk, jnp.broadcast_to(partial_value, (owners, 1))], axis=1),
        ((0, 0), (0, width2 - sub - 1)),
    )
    send2 = jnp.broadcast_to(rowdata[None], (replicas, owners, width2)).reshape(replicas * owners, width2)
    got2 = lax.all_to_all(send2, ("rep", "shard"), split_axis=0, concat_axis=0, tiled=True)
    got2 = got2.reshape(replicas, owners, width2)
    total = jnp.sum(got2[:, :, sub]) / (replicas * replicas)
    owned = (
        got2[:, :, :sub].transpose(1, 0, 2).reshape(owners, own_rows, cols).transpose(1, 0, 2)
    )
    main_len = own_rows * owners * cols
    grads = jnp.concatenate([owned.reshape(main_len), small_part]).reshape(1, -1)
    rms = jnp.sqrt(total / PARAMS)
    clip = jnp.minimum(1.0, 1.0 / (rms + clip_eps))
    clipped = grads * (clip / replicas)
    new_first = beta_one * first_moment + (1.0 - beta_one) * clipped
    new_second = beta_two * second_moment + (1.0 - beta_two) * clipped * clipped
    update = (
        new_first
        / (1.0 - beta_one**STEP)
        / (jnp.sqrt(new_second / (1.0 - beta_two**STEP)) + adam_eps)
    )
    column = jnp.arange(grads.shape[1], dtype=jnp.int32)[None, :]
    decayed = jnp.where(column < main_len, weight_decay * master_flat, 0.0)
    new_master = master_flat - learn_rate * (update + decayed)
    new_ema = ema_keep * ema_flat + (1.0 - ema_keep) * new_master
    weights = new_master[0, :main_len].astype(jnp.bfloat16)
    averaged = new_ema[0, :main_len].astype(jnp.bfloat16)
    stacked = jnp.stack([weights, averaged], axis=0).reshape(2, own_rows, owners, cols)
    back = stacked.transpose(2, 0, 1, 3).reshape(owners, 2 * piece)
    gains_mine = new_master[0, main_len:].astype(jnp.bfloat16)
    width2 = _pad_to(2 * piece + small)
    send2 = jnp.pad(
        jnp.concatenate([back, jnp.broadcast_to(gains_mine[None], (owners, small))], axis=1),
        ((0, 0), (0, width2 - 2 * piece - small)),
    )
    got2 = lax.all_to_all(send2, "shard", split_axis=0, concat_axis=0, tiled=True)
    weight_blocks = (
        got2[:, : 2 * piece].reshape(owners, 2, own_rows, cols).transpose(1, 0, 2, 3).reshape(2, rows, cols)
    )
    gains = got2[:, 2 * piece : 2 * piece + small].reshape(owners * small)
    return (new_first, new_second, new_master, new_ema, weight_blocks, gains)


def solution(mesh):
    return jax.shard_map(
        shards,
        mesh=mesh,
        in_specs=(
            P("rep", None, "shard"),
            P("rep", "shard"),
            P("shard", None),
            P("shard", None),
            P("shard", None),
            P("shard", None),
        ),
        out_specs=(
            P("shard", None),
            P("shard", None),
            P("shard", None),
            P("shard", None),
            P(None, None, "shard"),
            P(),
        ),
        check_vma=False,
    )
```

```python
import jax
import jax.numpy as jnp
from jax import lax
import functools

from jax.experimental import pallas as pl
from jax.experimental.pallas import tpu as pltpu
from jax.sharding import PartitionSpec as P

MESH = pl.DeviceIdType.MESH

STEP = 100
PARAMS = 3420672


beta_one = 0.9
beta_two = 0.95
adam_eps = 1e-08
learn_rate = 0.02
weight_decay = 0.1
ema_keep = 0.95
clip_eps = 1e-06

LANE = 128


def _pad_to(n):
    return -(-n // LANE) * LANE


def _rs_kernel(n, main, share, x_ref, o_ref, p_ref, recv, send_sem, recv_sem, local_sem):
    me = lax.axis_index("rep")
    shard = lax.axis_index("shard")
    barrier = pltpu.get_barrier_semaphore()
    for k in range(1, n):
        pl.semaphore_signal(barrier, inc=1, device_id=(lax.rem(me + k, n), shard), device_id_type=MESH)
    pl.semaphore_wait(barrier, n - 1)
    local = pltpu.make_async_copy(x_ref.at[me], recv.at[me], local_sem)
    local.start()

    def copy(k, j, src):
        return pltpu.make_async_remote_copy(
            src_ref=x_ref.at[j],
            dst_ref=recv.at[src],
            send_sem=send_sem.at[k],
            recv_sem=recv_sem.at[k],
            device_id=(j, shard),
            device_id_type=MESH,
        )

    for k in range(1, n):
        copy(k, lax.rem(me + k, n), me).start()
    local.wait()
    for k in range(1, n):
        c = copy(k, lax.rem(me + k, n), lax.rem(me + n - k, n))
        c.wait_send()
        c.wait_recv()
    total = recv[0]
    for k in range(1, n):
        total = total + recv[k]
    o_ref[...] = total
    flat = (
        lax.broadcasted_iota(jnp.int32, total.shape, 0) * total.shape[1]
        + lax.broadcasted_iota(jnp.int32, total.shape, 1)
    )
    start = main + me * share
    keep = (flat < main) | ((flat >= start) & (flat < start + share))
    squares = jnp.where(keep, total * total, 0.0)
    p_ref[...] = jnp.broadcast_to(jnp.sum(squares), p_ref.shape)


def reduce_scatter(x, main, share, collective_id):
    n, rows, lanes = x.shape
    return pl.pallas_call(
        functools.partial(_rs_kernel, n, main, share),
        out_shape=(
            jax.ShapeDtypeStruct((rows, lanes), x.dtype),
            jax.ShapeDtypeStruct((8, lanes), x.dtype),
        ),
        in_specs=[pl.BlockSpec(memory_space=pl.ANY)],
        out_specs=(pl.BlockSpec(memory_space=pltpu.VMEM), pl.BlockSpec(memory_space=pltpu.VMEM)),
        scratch_shapes=[
            pltpu.VMEM((n, rows, lanes), x.dtype),
            pltpu.SemaphoreType.DMA((n,)),
            pltpu.SemaphoreType.DMA((n,)),
            pltpu.SemaphoreType.DMA,
        ],
        compiler_params=pltpu.CompilerParams(collective_id=collective_id, has_side_effects=True),
    )(x)


def shards(grad_blocks, gain_grads, first_moment, second_moment, master_flat, ema_flat):
    replicas = lax.axis_size("rep")
    owners = lax.axis_size("shard")
    me = lax.axis_index("shard")
    rows, cols = grad_blocks.shape[1], grad_blocks.shape[2]
    small = gain_grads.shape[1]
    own_rows = rows // owners
    piece = own_rows * cols
    sub = piece // replicas
    gsub = small // replicas
    block = grad_blocks[0].reshape(owners, replicas, sub).transpose(1, 0, 2).reshape(replicas, owners * sub)
    gains_in = jnp.broadcast_to(gain_grads, (replicas, small))
    width = -(-(owners * sub + small) // (8 * LANE)) * 8 * LANE
    send = jnp.pad(jnp.concatenate([block, gains_in], axis=1), ((0, 0), (0, width - owners * sub - small)))
    mine, partial = reduce_scatter(send.reshape(replicas, width // LANE, LANE), owners * sub, gsub, 0)
    mine = mine.reshape(width)
    chunk = mine[: owners * sub].reshape(owners, sub)
    small_part = mine[owners * sub : owners * sub + small]
    partial_value = partial[0, 0]
    width2 = _pad_to(sub + 1)
    rowdata = jnp.pad(
        jnp.concatenate([chunk, jnp.broadcast_to(partial_value, (owners, 1))], axis=1),
        ((0, 0), (0, width2 - sub - 1)),
    )
    send2 = jnp.broadcast_to(rowdata[None], (replicas, owners, width2)).reshape(replicas * owners, width2)
    kept_first, kept_second, kept_ema = lax.optimization_barrier(
        (beta_one * first_moment, beta_two * second_moment, ema_keep * ema_flat)
    )
    got2 = lax.all_to_all(send2, ("rep", "shard"), split_axis=0, concat_axis=0, tiled=True)
    got2 = got2.reshape(replicas, owners, width2)
    total = jnp.sum(got2[:, :, sub]) / (replicas * replicas)
    owned = (
        got2[:, :, :sub].transpose(1, 0, 2).reshape(owners, own_rows, cols).transpose(1, 0, 2)
    )
    main_len = own_rows * owners * cols
    grads = jnp.concatenate([owned.reshape(main_len), small_part]).reshape(1, -1)
    rms = jnp.sqrt(total / PARAMS)
    clip = jnp.minimum(1.0, 1.0 / (rms + clip_eps))
    clipped = grads * (clip / replicas)
    new_first = kept_first + (1.0 - beta_one) * clipped
    new_second = kept_second + (1.0 - beta_two) * clipped * clipped
    update = (
        new_first
        / (1.0 - beta_one**STEP)
        / (jnp.sqrt(new_second / (1.0 - beta_two**STEP)) + adam_eps)
    )
    column = jnp.arange(grads.shape[1], dtype=jnp.int32)[None, :]
    decayed = jnp.where(column < main_len, weight_decay * master_flat, 0.0)
    new_master = master_flat - learn_rate * (update + decayed)
    new_ema = kept_ema + (1.0 - ema_keep) * new_master
    weights = new_master[0, :main_len].astype(jnp.bfloat16)
    averaged = new_ema[0, :main_len].astype(jnp.bfloat16)
    stacked = jnp.stack([weights, averaged], axis=0).reshape(2, own_rows, owners, cols)
    back = stacked.transpose(2, 0, 1, 3).reshape(owners, 2 * piece)
    gains_mine = new_master[0, main_len:].astype(jnp.bfloat16)
    width2 = _pad_to(2 * piece + small)
    send2 = jnp.pad(
        jnp.concatenate([back, jnp.broadcast_to(gains_mine[None], (owners, small))], axis=1),
        ((0, 0), (0, width2 - 2 * piece - small)),
    )
    got2 = lax.all_to_all(send2, "shard", split_axis=0, concat_axis=0, tiled=True)
    weight_blocks = (
        got2[:, : 2 * piece].reshape(owners, 2, own_rows, cols).transpose(1, 0, 2, 3).reshape(2, rows, cols)
    )
    gains = got2[:, 2 * piece : 2 * piece + small].reshape(owners * small)
    return (new_first, new_second, new_master, new_ema, weight_blocks, gains)


def solution(mesh):
    return jax.shard_map(
        shards,
        mesh=mesh,
        in_specs=(
            P("rep", None, "shard"),
            P("rep", "shard"),
            P("shard", None),
            P("shard", None),
            P("shard", None),
            P("shard", None),
        ),
        out_specs=(
            P("shard", None),
            P("shard", None),
            P("shard", None),
            P("shard", None),
            P(None, None, "shard"),
            P(),
        ),
        check_vma=False,
    )
```
